512 devices in a mesh: ang: 128 (over x, z, y_lo), rad: 4 (over y_hi, core).
Axes of the slice: x: 4, y: 8 (y_hi: 2, y_lo: 4; y = y_hi * 4 + y_lo), z: 8, core: 2. Of those that a mesh axis runs over, the one named last changes fastest.
Arguments:
- panel_slot: int32 [1048576], P(('ang', 'rad')), may hold values from 0 to 2047, as said below
- quad_points: float32 [9, 1048576], P(None, ('ang', 'rad')), may hold values from -27 to 27, as said below
- quad_weights: float32 [3, 1048576], P(None, ('ang', 'rad')), may hold values from 0.3 to 1
- densities: float32 [16, 1048576], P(None, ('ang', 'rad')), may hold values from -6 to 6
- near_pairs: int32 [128, 4, 4, 2, 4], P('ang', 'rad'), may hold values from 0 to 3, as said below
- quad_order: int32 [128, 4, 4, 4], P('ang', 'rad'), may hold values from 1 to 3, as said below
Outputs:
- potential: float32 [16, 1048576], P(None, ('ang', 'rad'))
The draws below stay inside these ranges and needn't reach their ends.
Inputs may be any that keep to these rules, and one draw needn't show every extreme that they name: `panel_slot`: each group of 2048 consecutive panels holds every slot 0 to 2047 once. `quad_points`: row 3 k + c holds coordinate c of quadrature point k. `near_pairs`: for each sector, band and link the 4 pairs are distinct; on link 3 every source block is 0 and the target blocks are 0 to 3, each once. `quad_order`: each entry is 1 or 3.
All inputs are finite; a program needn't handle non-finite values.
Results may differ from the reference program's by a relative error of at most 0.0003.
Values sent between devices are 32-bit elements; how exact they have to be, the bound alone decides.
A program may use at most 64 MiB of HBM per device.

```python
import math
import jax
import jax.numpy as jnp
from jax import lax

NCOL = 16
PAN = 2048
BLK = 512
LINKS = 4
SECTORS = 128
BANDS = 4
PANELS = 1048576


def slot_table(key):
    subkeys = jax.random.split(jax.random.fold_in(key, 11), SECTORS * BANDS)

    def permute(subkey):
        return jax.random.permutation(subkey, PAN)
    return jax.vmap(permute)(subkeys).reshape(-1).astype(jnp.int32)


def draw_panel_slot(key, part):
    return slot_table(key)


def draw_quad_points(key, part):
    slots = slot_table(key)
    panel = jnp.arange(PANELS, dtype=jnp.int32)
    device = panel // PAN
    sector = (device // BANDS).astype(jnp.float32)
    band = (device % BANDS).astype(jnp.float32)
    block = (slots // BLK).astype(jnp.float32)
    subkeys = jax.random.split(jax.random.fold_in(key, 23), 2)
    spread = jax.random.uniform(subkeys[0], (3, PANELS), jnp.float32)
    angle = 2.0 * math.pi * (sector + spread[0]) / SECTORS
    radius = SECTORS / (2.0 * math.pi) + band + (block + spread[1]) / (PAN // BLK)
    centre = jnp.stack([radius * jnp.cos(angle), radius * jnp.sin(angle), spread[2]])
    offsets = jnp.clip(0.05 * jax.random.normal(subkeys[1], (3, 3, PANELS), jnp.float32), -0.25, 0.25)
    return (centre[None] + offsets).reshape(9, PANELS).astype(jnp.float32)


def draw_near_pairs(key, part):
    devices = SECTORS * BANDS
    blocks = PAN // BLK
    cross_keys = jax.random.split(jax.random.fold_in(key, 31), devices * 3)

    def choose(subkey):
        return jax.random.permutation(subkey, blocks * blocks)[:blocks]
    picked = jax.vmap(choose)(cross_keys).reshape(devices, 3, blocks).astype(jnp.int32)
    cross = jnp.stack([picked // blocks, picked % blocks], axis=2)
    band_keys = jax.random.split(jax.random.fold_in(key, 37), devices)

    def order_blocks(subkey):
        return jax.random.permutation(subkey, blocks)
    targets = jax.vmap(order_blocks)(band_keys).astype(jnp.int32)
    radial = jnp.stack([targets, jnp.zeros_like(targets)], axis=1)[:, None]
    return jnp.concatenate([cross, radial], axis=1).reshape(SECTORS, BANDS, 4, 2, blocks).astype(jnp.int32)


def draw_quad_order(key, part):
    flags = jax.random.randint(jax.random.fold_in(key, 41), (SECTORS, BANDS, LINKS, PAN // BLK), 0, 2)
    orders = (1 + 2 * flags).astype(jnp.int32)
    return orders.at[0, 0, 0, 0].set(1).at[0, 0, 1, 0].set(3)


def shard_levels(stream_key, extent, shards, low, high):
    factor_of, own = 1.0, jax.random.fold_in(stream_key, 6)
    for position, shards_of in shards:
        steps = jnp.exp(jax.random.uniform(jax.random.fold_in(own, position), (shards_of,), jnp.float32, low / len(shards), high / len(shards)))
        factor_of = factor_of * jnp.repeat(steps, extent[position] // shards_of).reshape([-1 if axis == position else 1 for axis in range(len(extent))])
    return factor_of


def noise(rng, shape, scale, most, shards=(), kind=jnp.bfloat16):
    factor_of = shard_levels(rng, shape, shards, -0.22, 0.18) if shards else 1.0
    array = jax.random.normal(rng, shape, jnp.float32) * scale * factor_of
    return jnp.minimum(jnp.maximum(array, -most), most).astype(kind)


def setup_inputs(seed: int = 0) -> dict:
    streams_of = jax.random.split(jax.random.key(seed), 7)
    return {
        "panel_slot": draw_panel_slot(jax.random.fold_in(streams_of[6], 71), 0),
        "quad_points": draw_quad_points(jax.random.fold_in(streams_of[6], 71), 0),
        "quad_weights": jnp.clip(jnp.exp(math.log(1.0) - 1.2039728 * jax.random.uniform(streams_of[2], (3, PANELS), jnp.float32) ** shard_levels(streams_of[2], (3, PANELS), ((1, 512),), -0.2, 0.2)), 0.3, 1.0),
        "densities": noise(streams_of[3], (NCOL, PANELS), 1.0, 6.0, ((1, 512),), jnp.float32),
        "near_pairs": draw_near_pairs(jax.random.fold_in(streams_of[6], 71), 0),
        "quad_order": draw_quad_order(jax.random.fold_in(streams_of[6], 71), 0),
    }


softening = 0.01
green_scale = 0.25 / math.pi

def kernel_block(target_points, target_weights, source_points, source_weights, rule_order):
    target_area = target_weights[0] + target_weights[1] + target_weights[2]
    source_area = source_weights[0] + source_weights[1] + source_weights[2]
    soften = softening * (target_area[:, None] + source_area[None, :])

    def single(unused):
        distance = jnp.zeros_like(soften)
        for component in range(3):
            target_centre = (target_points[component] + target_points[3 + component] + target_points[6 + component]) / 3.0
            source_centre = (source_points[component] + source_points[3 + component] + source_points[6 + component]) / 3.0
            offset = target_centre[:, None] - source_centre[None, :]
            distance = distance + offset * offset
        return target_area[:, None] * source_area[None, :] * lax.rsqrt(distance + soften)

    def triple(unused):
        summed = jnp.zeros_like(soften)
        for target_point in range(3):
            for source_point in range(3):
                distance = jnp.zeros_like(soften)
                for component in range(3):
                    offset = target_points[3 * target_point + component][:, None] - source_points[3 * source_point + component][None, :]
                    distance = distance + offset * offset
                summed = summed + target_weights[target_point][:, None] * source_weights[source_point][None, :] * lax.rsqrt(distance + soften)
        return summed
    return green_scale * lax.cond(rule_order == 3, triple, single, 0)

def reference(panel_slot, quad_points, quad_weights, densities, near_pairs, quad_order):
    devices = SECTORS * BANDS
    slots = panel_slot.reshape(devices, PAN)

    def invert(slot_row):
        return jnp.zeros((PAN,), jnp.int32).at[slot_row].set(jnp.arange(PAN, dtype=jnp.int32))
    inverse = jax.vmap(invert)(slots)

    def pick(device_rows, slot_order):
        return device_rows[:, slot_order]

    def regroup(values):
        per_device = values.reshape(values.shape[0], devices, PAN).transpose(1, 0, 2)
        return jax.vmap(pick)(per_device, inverse)
    points = regroup(quad_points)
    weights = regroup(quad_weights)
    density = regroup(densities)
    pair_table = near_pairs.reshape(devices, LINKS, 2, PAN // BLK)
    order_table = quad_order.reshape(devices, LINKS, PAN // BLK)
    zero = jnp.int32(0)

    def cut(values, device, start):
        return lax.dynamic_slice(values, (device, zero, start), (1, values.shape[1], BLK))[0]

    def device_step(device, result):
        device = jnp.asarray(device).astype(jnp.int32)
        sector = device // BANDS
        band = device % BANDS
        partners = (device, (sector + 1) % SECTORS * BANDS + band, (sector + 2) % SECTORS * BANDS + band, sector * BANDS + jnp.minimum(band + 1, BANDS - 1))
        present = jnp.where(band + 1 < BANDS, 1.0, 0.0).astype(jnp.float32)
        for link_index in range(LINKS):
            partner = partners[link_index]

            def pair_step(entry, result_now):
                target_start = (pair_table[device, link_index, 0, entry] * BLK).astype(jnp.int32)
                source_start = (pair_table[device, link_index, 1, entry] * BLK).astype(jnp.int32)
                tile = kernel_block(cut(points, device, target_start), cut(weights, device, target_start), cut(points, partner, source_start), cut(weights, partner, source_start), order_table[device, link_index, entry])
                if link_index == 3:
                    tile = tile * present
                forward = jnp.dot(cut(density, partner, source_start), tile.T, precision=lax.Precision.HIGHEST, preferred_element_type=jnp.float32)
                current = cut(result_now, device, target_start)
                result_now = lax.dynamic_update_slice(result_now, (current + forward)[None], (device, zero, target_start))
                if link_index > 0:
                    backward = jnp.dot(cut(density, device, target_start), tile, precision=lax.Precision.HIGHEST, preferred_element_type=jnp.float32)
                    current = cut(result_now, partner, source_start)
                    result_now = lax.dynamic_update_slice(result_now, (current + backward)[None], (partner, zero, source_start))
                return result_now
            result = lax.fori_loop(0, PAN // BLK, pair_step, result)
        return result
    result = lax.fori_loop(0, devices, device_step, jnp.zeros((devices, NCOL, PAN), jnp.float32))
    ordered = jax.vmap(pick)(result, slots)
    return ordered.transpose(1, 0, 2).reshape(NCOL, devices * PAN)
```

```python
import math

import jax
import jax.numpy as jnp
from jax import lax
from jax.experimental import pallas as pl
from jax.experimental.pallas import tpu as pltpu
from jax.sharding import PartitionSpec as P

NCOL = 16
PAN = 2048
BLK = 512
NBLK = PAN // BLK
ROWS = 32
DEPTH = 128
HALF = 256
MESH = pl.DeviceIdType.MESH
F32 = jnp.float32
BF16 = jnp.bfloat16

softening = 0.01
green_scale = 0.25 / math.pi

MINOR = (((1,), (1,)), ((), ()))


def split3(value):
    high = value.astype(BF16).astype(F32)
    rest = value - high
    middle = rest.astype(BF16).astype(F32)
    return high, middle, rest - middle


def dot(a, b):
    return jnp.dot(a, b, preferred_element_type=F32)


def dot_minor(a, b):
    return lax.dot_general(a, b, MINOR, preferred_element_type=F32)


def parts_of(raw_ref, variant, count):
    first, second, third = (raw_ref[pl.ds(16 + 3 * k, 3), :] for k in range(3))
    w = raw_ref[pl.ds(25, 3), :]
    area = w[0:1] + w[1:2] + w[2:3]
    if variant < 3:
        x = (first, second, third)[variant]
        weight = w[variant : variant + 1]
    else:
        x = (first + second + third) / 3.0
        weight = area / 3.0
    a = jnp.round(x * 8.0) * 0.125
    rest = x - a
    b = rest.astype(BF16).astype(F32)
    c = (rest - b).astype(BF16).astype(F32)
    fine = b + c
    square = jnp.sum(a * a, axis=0, keepdims=True)
    linear = jnp.sum(2.0 * a * fine + fine * fine, axis=0, keepdims=True) + softening * area
    return a, b, c, split3(square), split3(linear), weight


def stage_source(stage, raw_ref, variant, count):
    a, b, c, square, linear, weight = parts_of(raw_ref, variant, count)
    cols = slice(0, count)
    stage[0:3, cols] = -2.0 * a
    ones = jnp.ones((3, count), F32)
    for row, values in ((8, square), (16, linear)):
        stage[row : row + 3, cols] = ones
        for index in range(3):
            stage[row + 3 + index : row + 4 + index, cols] = values[index]
    for row, value in ((24, b), (32, c), (40, a), (48, a), (56, b), (64, c), (72, b), (80, c)):
        stage[row : row + 3, cols] = -2.0 * value
    return weight


def stage_target(stage, raw_ref, variant, count):
    a, b, c, square, linear, weight = parts_of(raw_ref, variant, count)
    stage[0:3, :] = a
    ones = jnp.ones((3, count), F32)
    for row, values in ((8, square), (16, linear)):
        stage[row + 3 : row + 6, :] = ones
        for index in range(3):
            stage[row + index : row + 1 + index, :] = values[index]
    for row, value in ((24, a), (32, a), (40, b), (48, c), (56, b), (64, b), (72, c), (80, c)):
        stage[row : row + 3, :] = value
    for index, value in enumerate(split3(weight * green_scale)):
        stage[88 + index : 89 + index, :] = value


def kernel(
    sectors,
    bands,
    pair_ref,
    order_ref,
    slot_ref,
    points_ref,
    weights_ref,
    densities_ref,
    out_ref,
    onehot,
    raw,
    near1,
    near2,
    edge,
    stage,
    target,
    target_weight,
    source,
    source_weight,
    density,
    tile_high,
    tile_low,
    result,
    sent1,
    sent2,
    sent3,
    back1,
    back2,
    back3,
    send_sem,
    recv_sem,
):
    sector = lax.axis_index("ang")
    band = lax.axis_index("rad")

    def at_sector(step):
        return (lax.rem(sector + step + sectors, sectors), band)

    inner = (sector, jnp.maximum(band - 1, 0))
    outer = (sector, jnp.minimum(band + 1, bands - 1))
    has_inner = band > 0
    has_outer = band < bands - 1

    def remote(src, dst, index, device):
        return pltpu.make_async_remote_copy(
            src_ref=src,
            dst_ref=dst,
            send_sem=send_sem.at[index],
            recv_sem=recv_sem.at[index],
            device_id=device,
            device_id_type=MESH,
        )

    out1 = remote(raw, near1, 0, at_sector(-1))
    out2 = remote(raw, near2, 1, at_sector(-2))
    out3 = remote(raw.at[:, pl.ds(0, BLK)], edge, 2, inner)
    ret1 = remote(sent1, back1, 3, at_sector(1))
    ret2 = remote(sent2, back2, 4, at_sector(2))
    ret3 = remote(sent3, back3, 5, outer)

    barrier = pltpu.get_barrier_semaphore()
    for step in (-2, -1, 1, 2):
        pl.semaphore_signal(barrier, inc=1, device_id=at_sector(step), device_id_type=MESH)

    @pl.when(has_inner)
    def _():
        pl.semaphore_signal(barrier, inc=1, device_id=inner, device_id_type=MESH)

    @pl.when(has_outer)
    def _():
        pl.semaphore_signal(barrier, inc=1, device_id=outer, device_id_type=MESH)

    slots = slot_ref[...]
    values = jnp.concatenate(
        [densities_ref[...], points_ref[...], weights_ref[...], jnp.zeros((4, PAN), F32)], axis=0
    )
    pieces = jnp.concatenate([piece.astype(BF16) for piece in split3(values)], axis=0)

    def permute(block, carry):
        rows = pl.ds(pl.multiple_of(block * HALF, HALF), HALF)
        index = lax.broadcasted_iota(jnp.int32, (HALF, PAN), 0) + block * HALF
        hot = jnp.where(index == slots, 1.0, 0.0).astype(BF16)
        onehot[rows, :] = hot
        moved = dot_minor(pieces, hot)
        raw[:, rows] = moved[0:32] + moved[32:64] + moved[64:96]
        return carry

    lax.fori_loop(0, PAN // HALF, permute, 0)

    pl.semaphore_wait(barrier, 4 + jnp.minimum(band, 1) + jnp.minimum(bands - 1 - band, 1))

    @pl.when(has_inner)
    def _():
        out3.start()

    out2.start()
    out1.start()

    stage[...] = jnp.zeros_like(stage)
    pick = jnp.where(
        jnp.logical_and(
            lax.broadcasted_iota(jnp.int32, (DEPTH, 128), 0) >= 88,
            lax.broadcasted_iota(jnp.int32, (DEPTH, 128), 0) < 91,
        ),
        1.0,
        0.0,
    ).astype(BF16)
    for variant in range(4):
        stage_target(stage, raw, variant, PAN)
        for index in range(NBLK):
            turned = stage[:, index * BLK : (index + 1) * BLK].T.astype(BF16)
            target[4 * index + variant] = turned
            target_weight[4 * index + variant] = dot(turned, pick)
    stage[...] = jnp.zeros_like(stage)

    def load_source(link, raw_ref, count):
        for variant in range(4):
            weight = stage_source(stage, raw_ref, variant, count)
            for index in range(count // HALF):
                cols = slice(index * HALF, (index + 1) * HALF)
                place = ((link * NBLK + index // 2) * 4 + variant) * 2 + index % 2
                source[place] = stage[:, cols].astype(BF16)
                source_weight[place] = weight[:, cols]
        for index in range(count // BLK):
            d = raw_ref[0:16, index * BLK : (index + 1) * BLK]
            high = d.astype(BF16)
            density[link * NBLK + index, 0:16, :] = high
            density[link * NBLK + index, 16:32, :] = (d - high.astype(F32)).astype(BF16)

    load_source(0, raw, PAN)
    result[...] = jnp.zeros_like(result)
    sent1[...] = jnp.zeros_like(sent1)
    sent2[...] = jnp.zeros_like(sent2)
    sent3[...] = jnp.zeros_like(sent3)

    def tile(step, carry):
        link = lax.rem(3 * lax.div(step + 3, 4), 4)
        entry = lax.rem(step + 3, 4)

        @pl.when(jnp.logical_and(step == 1, has_outer))
        def _():
            out3.wait_recv()
            load_source(3, edge, BLK)

        @pl.when(step == 5)
        def _():
            @pl.when(has_outer)
            def _():
                ret3.start()

            out2.wait_recv()
            load_source(2, near2, PAN)

        @pl.when(step == 9)
        def _():
            ret2.start()
            out1.wait_recv()
            load_source(1, near1, PAN)

        @pl.when(step == 13)
        def _():
            ret1.start()

        @pl.when(jnp.logical_or(link != 3, has_outer))
        def _():
            target_block = pair_ref[link * 8 + entry]
            source_block = pair_ref[link * 8 + 4 + entry]
            order = order_ref[link * 4 + entry]
            variants = [jnp.where(order == 3, k, 3) for k in range(3)]
            source_place = link * NBLK + source_block
            for half in range(BLK // HALF):
                block = None
                for k in range(3):
                    points = target[4 * target_block + variants[k]]
                    inner_sum = None
                    for l in range(3):
                        place = (4 * source_place + variants[l]) * 2 + half
                        term = lax.rsqrt(dot(points, source[place])) * source_weight[place]
                        inner_sum = term if inner_sum is None else inner_sum + term
                    scale = target_weight[4 * target_block + variants[k]]
                    term = inner_sum * jnp.concatenate([scale, scale], axis=1)
                    block = term if block is None else block + term
                high = block.astype(BF16)
                tile_high[:, half * HALF : (half + 1) * HALF] = high
                tile_low[:, half * HALF : (half + 1) * HALF] = (block - high.astype(F32)).astype(BF16)
            high = tile_high[...]
            low = tile_low[...]
            far = density[source_place]
            full = dot_minor(far, high)
            forward = full[0:16] + full[16:32] + dot_minor(far[0:16], low)
            for index in range(NBLK):
                result[index] = result[index] + jnp.where(target_block == index, forward, 0.0)

            @pl.when(link != 0)
            def _():
                own = density[target_block]
                full = dot(own, high)
                backward = full[0:16] + full[16:32] + dot(own[0:16], low)

                @pl.when(link == 1)
                def _():
                    for index in range(NBLK):
                        sent1[index] = sent1[index] + jnp.where(source_block == index, backward, 0.0)

                @pl.when(link == 2)
                def _():
                    for index in range(NBLK):
                        sent2[index] = sent2[index] + jnp.where(source_block == index, backward, 0.0)

                @pl.when(link == 3)
                def _():
                    sent3[...] = sent3[...] + backward

        return carry

    lax.fori_loop(0, 16, tile, 0)

    @pl.when(has_inner)
    def _():
        ret3.wait_recv()
        result[0] = result[0] + back3[...]

    ret1.wait_recv()
    ret2.wait_recv()
    total = jnp.zeros((3 * NCOL, PAN), F32)
    for index in range(NBLK):
        block = result[index] + back1[index] + back2[index]
        moved = jnp.concatenate([piece.astype(BF16) for piece in split3(block)], axis=0)
        total = total + dot(moved, onehot[index * BLK : (index + 1) * BLK, :])
    out_ref[...] = total[0:16] + total[16:32] + total[32:48]

    out1.wait_send()
    out2.wait_send()
    ret1.wait_send()
    ret2.wait_send()

    @pl.when(has_inner)
    def _():
        out3.wait_send()

    @pl.when(has_outer)
    def _():
        ret3.wait_send()


def solution(mesh):
    sectors, bands = mesh.shape["ang"], mesh.shape["rad"]

    def on_device(panel_slot, quad_points, quad_weights, densities, near_pairs, quad_order):
        vmem = pl.BlockSpec(memory_space=pltpu.VMEM)
        smem = pl.BlockSpec(memory_space=pltpu.SMEM)

        def body(*refs):
            kernel(sectors, bands, *refs)

        return pl.pallas_call(
            body,
            name="near_field",
            out_shape=jax.ShapeDtypeStruct((NCOL, PAN), F32),
            in_specs=[smem, smem, vmem, vmem, vmem, vmem],
            out_specs=vmem,
            scratch_shapes=[
                pltpu.VMEM((PAN, PAN), BF16),
                pltpu.VMEM((ROWS, PAN), F32),
                pltpu.VMEM((ROWS, PAN), F32),
                pltpu.VMEM((ROWS, PAN), F32),
                pltpu.VMEM((ROWS, BLK), F32),
                pltpu.VMEM((DEPTH, PAN), F32),
                pltpu.VMEM((NBLK * 4, BLK, DEPTH), BF16),
                pltpu.VMEM((NBLK * 4, BLK, 128), F32),
                pltpu.VMEM((4 * NBLK * 8, DEPTH, HALF), BF16),
                pltpu.VMEM((4 * NBLK * 8, 1, HALF), F32),
                pltpu.VMEM((4 * NBLK, 2 * NCOL, BLK), BF16),
                pltpu.VMEM((BLK, BLK), BF16),
                pltpu.VMEM((BLK, BLK), BF16),
                pltpu.VMEM((NBLK, NCOL, BLK), F32),
                pltpu.VMEM((NBLK, NCOL, BLK), F32),
                pltpu.VMEM((NBLK, NCOL, BLK), F32),
                pltpu.VMEM((NCOL, BLK), F32),
                pltpu.VMEM((NBLK, NCOL, BLK), F32),
                pltpu.VMEM((NBLK, NCOL, BLK), F32),
                pltpu.VMEM((NCOL, BLK), F32),
                pltpu.SemaphoreType.DMA((6,)),
                pltpu.SemaphoreType.DMA((6,)),
            ],
            compiler_params=pltpu.CompilerParams(
                collective_id=0, has_side_effects=True, vmem_limit_bytes=60 * 1024 * 1024
            ),
        )(
            near_pairs.reshape(-1),
            quad_order.reshape(-1),
            panel_slot.reshape(1, PAN),
            quad_points,
            quad_weights,
            densities,
        )

    return jax.shard_map(
        on_device,
        mesh=mesh,
        in_specs=(
            P(("ang", "rad")),
            P(None, ("ang", "rad")),
            P(None, ("ang", "rad")),
            P(None, ("ang", "rad")),
            P("ang", "rad", None, None, None),
            P("ang", "rad", None, None),
        ),
        out_specs=P(None, ("ang", "rad")),
        check_vma=False,
    )
```

```python
import math

import jax
import jax.numpy as jnp
from jax import lax
from jax.experimental import pallas as pl
from jax.experimental.pallas import tpu as pltpu
from jax.sharding import PartitionSpec as P

NCOL = 16
PAN = 2048
BLK = 512
NBLK = PAN // BLK
ROWS = 28
DEPTH = 128
HALF = 256
MESH = pl.DeviceIdType.MESH
F32 = jnp.float32
BF16 = jnp.bfloat16

softening = 0.01
green_scale = 0.25 / math.pi

MINOR = (((1,), (1,)), ((), ()))


def split3(value):
    high = value.astype(BF16).astype(F32)
    rest = value - high
    middle = rest.astype(BF16).astype(F32)
    return high, middle, rest - middle


def dot(a, b):
    return jnp.dot(a, b, preferred_element_type=F32)


def dot_minor(a, b):
    return lax.dot_general(a, b, MINOR, preferred_element_type=F32)


def parts_of(raw_ref, variant, count):
    first, second, third = (raw_ref[pl.ds(16 + 3 * k, 3), :] for k in range(3))
    w = raw_ref[pl.ds(25, 3), :]
    area = w[0:1] + w[1:2] + w[2:3]
    if variant < 3:
        x = (first, second, third)[variant]
        weight = w[variant : variant + 1]
    else:
        x = (first + second + third) / 3.0
        weight = area / 3.0
    a = jnp.round(x * 8.0) * 0.125
    rest = x - a
    b = rest.astype(BF16).astype(F32)
    c = (rest - b).astype(BF16).astype(F32)
    fine = b + c
    square = jnp.sum(a * a, axis=0, keepdims=True)
    linear = jnp.sum(2.0 * a * fine + fine * fine, axis=0, keepdims=True) + softening * area
    return a, b, c, split3(square), split3(linear), weight


def stage_source(stage, raw_ref, variant, count):
    a, b, c, square, linear, weight = parts_of(raw_ref, variant, count)
    cols = slice(0, count)
    stage[0:3, cols] = -2.0 * a
    ones = jnp.ones((3, count), F32)
    for row, values in ((8, square), (16, linear)):
        stage[row : row + 3, cols] = ones
        for index in range(3):
            stage[row + 3 + index : row + 4 + index, cols] = values[index]
    for row, value in ((24, b), (32, c), (40, a), (48, a), (56, b), (64, c), (72, b), (80, c)):
        stage[row : row + 3, cols] = -2.0 * value
    return weight


def stage_target(stage, raw_ref, variant, count):
    a, b, c, square, linear, weight = parts_of(raw_ref, variant, count)
    stage[0:3, :] = a
    ones = jnp.ones((3, count), F32)
    for row, values in ((8, square), (16, linear)):
        stage[row + 3 : row + 6, :] = ones
        for index in range(3):
            stage[row + index : row + 1 + index, :] = values[index]
    for row, value in ((24, a), (32, a), (40, b), (48, c), (56, b), (64, b), (72, c), (80, c)):
        stage[row : row + 3, :] = value
    for index, value in enumerate(split3(weight * green_scale)):
        stage[88 + index : 89 + index, :] = value


def kernel(
    sectors,
    bands,
    pair_ref,
    order_ref,
    slot_ref,
    points_ref,
    weights_ref,
    densities_ref,
    out_ref,
    raw,
    near1,
    near2,
    edge,
    stage,
    target,
    target_weight,
    source,
    source_weight,
    density,
    tile_high,
    tile_low,
    result,
    sent1,
    sent2,
    sent3,
    back1,
    back2,
    back3,
    send_sem,
    recv_sem,
):
    sector = lax.axis_index("ang")
    band = lax.axis_index("rad")

    def at_sector(step):
        return (lax.rem(sector + step + sectors, sectors), band)

    inner = (sector, jnp.maximum(band - 1, 0))
    outer = (sector, jnp.minimum(band + 1, bands - 1))
    has_inner = band > 0
    has_outer = band < bands - 1

    def remote(src, dst, index, device):
        return pltpu.make_async_remote_copy(
            src_ref=src,
            dst_ref=dst,
            send_sem=send_sem.at[index],
            recv_sem=recv_sem.at[index],
            device_id=device,
            device_id_type=MESH,
        )

    out1 = remote(raw, near1, 0, at_sector(-1))
    relay = remote(near1, near2, 1, at_sector(-1))
    out3 = remote(raw.at[:, pl.ds(0, BLK)], edge, 2, inner)
    ret1 = remote(sent1, back1, 3, at_sector(1))
    ret2 = remote(sent2, back2, 4, at_sector(2))
    ret3 = remote(sent3, back3, 5, outer)

    barrier = pltpu.get_barrier_semaphore()
    for step in (-2, -1, 1, 2):
        pl.semaphore_signal(barrier, inc=1, device_id=at_sector(step), device_id_type=MESH)

    @pl.when(has_inner)
    def _():
        pl.semaphore_signal(barrier, inc=1, device_id=inner, device_id_type=MESH)

    @pl.when(has_outer)
    def _():
        pl.semaphore_signal(barrier, inc=1, device_id=outer, device_id_type=MESH)

    slots = slot_ref[...]
    values = jnp.concatenate(
        [densities_ref[...], points_ref[...], weights_ref[...], jnp.zeros((32 - ROWS, PAN), F32)], axis=0
    )
    pieces = jnp.concatenate([piece.astype(BF16) for piece in split3(values)], axis=0)

    def permute(block, carry):
        rows = pl.ds(pl.multiple_of(block * HALF, HALF), HALF)
        index = lax.broadcasted_iota(jnp.int32, (HALF, PAN), 0) + block * HALF
        hot = jnp.where(index == slots, 1.0, 0.0).astype(BF16)
        moved = dot_minor(pieces, hot)
        raw[:, rows] = (moved[0:32] + moved[32:64] + moved[64:96])[0:ROWS]
        return carry

    lax.fori_loop(0, PAN // HALF, permute, 0)

    stage[...] = jnp.zeros_like(stage)
    pick = jnp.where(
        jnp.logical_and(
            lax.broadcasted_iota(jnp.int32, (DEPTH, 128), 0) >= 88,
            lax.broadcasted_iota(jnp.int32, (DEPTH, 128), 0) < 91,
        ),
        1.0,
        0.0,
    ).astype(BF16)
    for variant in range(4):
        stage_target(stage, raw, variant, PAN)
        for index in range(NBLK):
            turned = stage[:, index * BLK : (index + 1) * BLK].T.astype(BF16)
            target[4 * index + variant] = turned
            target_weight[4 * index + variant] = dot(turned, pick)
    pl.semaphore_wait(barrier, 4 + jnp.minimum(band, 1) + jnp.minimum(bands - 1 - band, 1))

    out1.start()

    @pl.when(has_inner)
    def _():
        out3.start()


    stage[...] = jnp.zeros_like(stage)

    def load_source(link, raw_ref, count):
        for variant in range(4):
            weight = stage_source(stage, raw_ref, variant, count)
            for index in range(count // HALF):
                cols = slice(index * HALF, (index + 1) * HALF)
                place = ((link * NBLK + index // 2) * 4 + variant) * 2 + index % 2
                source[place] = stage[:, cols].astype(BF16)
                source_weight[place] = weight[:, cols]
        for index in range(count // BLK):
            d = raw_ref[0:16, index * BLK : (index + 1) * BLK]
            high = d.astype(BF16)
            density[link * NBLK + index, 0:16, :] = high
            density[link * NBLK + index, 16:32, :] = (d - high.astype(F32)).astype(BF16)

    load_source(0, raw, PAN)
    result[...] = jnp.zeros_like(result)
    sent1[...] = jnp.zeros_like(sent1)
    sent2[...] = jnp.zeros_like(sent2)
    sent3[...] = jnp.zeros_like(sent3)

    def tile(step, carry):
        link = lax.rem(lax.div(step + 2, 4), 4)
        entry = lax.rem(step + 2, 4)

        @pl.when(step == 2)
        def _():
            out1.wait_recv()
            relay.start()
            load_source(1, near1, PAN)

        @pl.when(step == 6)
        def _():
            ret1.start()
            relay.wait_recv()
            load_source(2, near2, PAN)

        @pl.when(step == 10)
        def _():
            ret2.start()

            @pl.when(has_outer)
            def _():
                out3.wait_recv()
                load_source(3, edge, BLK)

        @pl.when(jnp.logical_and(step == 14, has_outer))
        def _():
            ret3.start()

        @pl.when(jnp.logical_or(link != 3, has_outer))
        def _():
            target_block = pair_ref[0, 0, link, 0, entry]
            source_block = pair_ref[0, 0, link, 1, entry]
            order = order_ref[0, 0, link, entry]
            variants = [jnp.where(order == 3, k, 3) for k in range(3)]
            source_place = link * NBLK + source_block
            for half in range(BLK // HALF):
                block = None
                for k in range(3):
                    points = target[4 * target_block + variants[k]]
                    inner_sum = None
                    for l in range(3):
                        place = (4 * source_place + variants[l]) * 2 + half
                        term = lax.rsqrt(dot(points, source[place])) * source_weight[place]
                        inner_sum = term if inner_sum is None else inner_sum + term
                    scale = target_weight[4 * target_block + variants[k]]
                    term = inner_sum * jnp.concatenate([scale, scale], axis=1)
                    block = term if block is None else block + term
                high = block.astype(BF16)
                tile_high[:, half * HALF : (half + 1) * HALF] = high
                tile_low[:, half * HALF : (half + 1) * HALF] = (block - high.astype(F32)).astype(BF16)
            high = tile_high[...]
            low = tile_low[...]
            far = density[source_place]
            full = dot_minor(far, high)
            forward = full[0:16] + full[16:32] + dot_minor(far[0:16], low)
            for index in range(NBLK):
                result[index] = result[index] + jnp.where(target_block == index, forward, 0.0)

            @pl.when(link != 0)
            def _():
                own = density[target_block]
                full = dot(own, high)
                backward = full[0:16] + full[16:32] + dot(own[0:16], low)

                @pl.when(link == 1)
                def _():
                    for index in range(NBLK):
                        sent1[index] = sent1[index] + jnp.where(source_block == index, backward, 0.0)

                @pl.when(link == 2)
                def _():
                    for index in range(NBLK):
                        sent2[index] = sent2[index] + jnp.where(source_block == index, backward, 0.0)

                @pl.when(link == 3)
                def _():
                    sent3[...] = sent3[...] + backward

        return carry

    lax.fori_loop(0, 16, tile, 0)

    @pl.when(has_inner)
    def _():
        ret3.wait_recv()
        result[0] = result[0] + back3[...]

    ret1.wait_recv()
    ret2.wait_recv()
    for index in range(NBLK):
        out_ref[:, index * BLK : (index + 1) * BLK] = result[index] + back1[index] + back2[index]

    out1.wait_send()
    relay.wait_send()
    ret1.wait_send()
    ret2.wait_send()

    @pl.when(has_inner)
    def _():
        out3.wait_send()

    @pl.when(has_outer)
    def _():
        ret3.wait_send()


def restore(slot_ref, value_ref, out_ref):
    lanes = 128
    for first in range(0, PAN, lanes):
        slots = jnp.broadcast_to(slot_ref[:, first : first + lanes], (NCOL, lanes))
        lane = jnp.bitwise_and(slots, lanes - 1)
        group = jnp.right_shift(slots, 7)
        total = jnp.zeros((NCOL, lanes), F32)
        for index in range(PAN // lanes):
            part = value_ref[:, index * lanes : (index + 1) * lanes]
            found = jnp.take_along_axis(part, lane, axis=1, mode="promise_in_bounds")
            total = jnp.where(group == index, found, total)
        out_ref[:, first : first + lanes] = total


def solution(mesh):
    sectors, bands = mesh.shape["ang"], mesh.shape["rad"]

    def on_device(panel_slot, quad_points, quad_weights, densities, near_pairs, quad_order):
        vmem = pl.BlockSpec(memory_space=pltpu.VMEM)
        smem = pl.BlockSpec(memory_space=pltpu.SMEM)

        def body(*refs):
            kernel(sectors, bands, *refs)

        slots = panel_slot.reshape(1, PAN)
        ordered = pl.pallas_call(
            body,
            name="near_field",
            out_shape=jax.ShapeDtypeStruct((NCOL, PAN), F32),
            in_specs=[smem, smem, vmem, vmem, vmem, vmem],
            out_specs=vmem,
            scratch_shapes=[
                pltpu.VMEM((ROWS, PAN), F32),
                pltpu.VMEM((ROWS, PAN), F32),
                pltpu.VMEM((ROWS, PAN), F32),
                pltpu.VMEM((ROWS, BLK), F32),
                pltpu.VMEM((DEPTH, PAN), F32),
                pltpu.VMEM((NBLK * 4, BLK, DEPTH), BF16),
                pltpu.VMEM((NBLK * 4, BLK, 128), F32),
                pltpu.VMEM((4 * NBLK * 8, DEPTH, HALF), BF16),
                pltpu.VMEM((4 * NBLK * 8, 1, HALF), F32),
                pltpu.VMEM((4 * NBLK, 2 * NCOL, BLK), BF16),
                pltpu.VMEM((BLK, BLK), BF16),
                pltpu.VMEM((BLK, BLK), BF16),
                pltpu.VMEM((NBLK, NCOL, BLK), F32),
                pltpu.VMEM((NBLK, NCOL, BLK), F32),
                pltpu.VMEM((NBLK, NCOL, BLK), F32),
                pltpu.VMEM((NCOL, BLK), F32),
                pltpu.VMEM((NBLK, NCOL, BLK), F32),
                pltpu.VMEM((NBLK, NCOL, BLK), F32),
                pltpu.VMEM((NCOL, BLK), F32),
                pltpu.SemaphoreType.DMA((6,)),
                pltpu.SemaphoreType.DMA((6,)),
            ],
            compiler_params=pltpu.CompilerParams(
                collective_id=0, has_side_effects=True, vmem_limit_bytes=60 * 1024 * 1024
            ),
        )(
            near_pairs,
            quad_order,
            slots,
            quad_points,
            quad_weights,
            densities,
        )
        return pl.pallas_call(
            restore,
            name="restore",
            out_shape=jax.ShapeDtypeStruct((NCOL, PAN), F32),
            in_specs=[vmem, vmem],
            out_specs=vmem,
        )(slots, ordered)

    return jax.shard_map(
        on_device,
        mesh=mesh,
        in_specs=(
            P(("ang", "rad")),
            P(None, ("ang", "rad")),
            P(None, ("ang", "rad")),
            P(None, ("ang", "rad")),
            P("ang", "rad", None, None, None),
            P("ang", "rad", None, None),
        ),
        out_specs=P(None, ("ang", "rad")),
        check_vma=False,
    )
```

```python
import math

import jax
import jax.numpy as jnp
from jax import lax
from jax.experimental import pallas as pl
from jax.experimental.pallas import tpu as pltpu
from jax.sharding import PartitionSpec as P

NCOL = 16
PAN = 2048
BLK = 512
NBLK = PAN // BLK
ROWS = 28
DEPTH = 128
HALF = 256
MESH = pl.DeviceIdType.MESH
F32 = jnp.float32
BF16 = jnp.bfloat16

softening = 0.01
green_scale = 0.25 / math.pi

MINOR = (((1,), (1,)), ((), ()))


def split3(value):
    high = value.astype(BF16).astype(F32)
    rest = value - high
    middle = rest.astype(BF16).astype(F32)
    return high, middle, rest - middle


def dot(a, b):
    return jnp.dot(a, b, preferred_element_type=F32)


def dot_minor(a, b):
    return lax.dot_general(a, b, MINOR, preferred_element_type=F32)


def parts_of(raw_ref, variant, count):
    first, second, third = (raw_ref[pl.ds(16 + 3 * k, 3), :] for k in range(3))
    w = raw_ref[pl.ds(25, 3), :]
    area = w[0:1] + w[1:2] + w[2:3]
    if variant < 3:
        x = (first, second, third)[variant]
        weight = w[variant : variant + 1]
    else:
        x = (first + second + third) / 3.0
        weight = area / 3.0
    a = jnp.round(x * 8.0) * 0.125
    rest = x - a
    b = rest.astype(BF16).astype(F32)
    c = (rest - b).astype(BF16).astype(F32)
    fine = b + c
    square = jnp.sum(a * a, axis=0, keepdims=True)
    linear = jnp.sum(2.0 * a * fine + fine * fine, axis=0, keepdims=True) + softening * area
    return a, b, c, split3(square), split3(linear), weight


def stage_source(stage, raw_ref, variant, count):
    a, b, c, square, linear, weight = parts_of(raw_ref, variant, count)
    cols = slice(0, count)
    stage[0:3, cols] = -2.0 * a
    ones = jnp.ones((3, count), F32)
    for row, values in ((8, square), (16, linear)):
        stage[row : row + 3, cols] = ones
        for index in range(3):
            stage[row + 3 + index : row + 4 + index, cols] = values[index]
    for row, value in ((24, b), (32, c), (40, a), (48, a), (56, b), (64, c), (72, b), (80, c)):
        stage[row : row + 3, cols] = -2.0 * value
    return weight


def stage_target(stage, raw_ref, variant, count):
    a, b, c, square, linear, weight = parts_of(raw_ref, variant, count)
    stage[0:3, :] = a
    ones = jnp.ones((3, count), F32)
    for row, values in ((8, square), (16, linear)):
        stage[row + 3 : row + 6, :] = ones
        for index in range(3):
            stage[row + index : row + 1 + index, :] = values[index]
    for row, value in ((24, a), (32, a), (40, b), (48, c), (56, b), (64, b), (72, c), (80, c)):
        stage[row : row + 3, :] = value
    for index, value in enumerate(split3(weight * green_scale)):
        stage[88 + index : 89 + index, :] = value


def kernel(
    sectors,
    bands,
    pair_ref,
    order_ref,
    slot_ref,
    points_ref,
    weights_ref,
    densities_ref,
    out_ref,
    raw,
    near1,
    near2,
    edge,
    stage,
    target,
    target_weight,
    source,
    source_weight,
    density,
    tile_high,
    tile_low,
    result,
    sent1,
    sent2,
    sent3,
    back1,
    back2,
    back3,
    send_sem,
    recv_sem,
):
    sector = lax.axis_index("ang")
    band = lax.axis_index("rad")

    def at_sector(step):
        return (lax.rem(sector + step + sectors, sectors), band)

    inner = (sector, jnp.maximum(band - 1, 0))
    outer = (sector, jnp.minimum(band + 1, bands - 1))
    has_inner = band > 0
    has_outer = band < bands - 1

    def remote(src, dst, index, device):
        return pltpu.make_async_remote_copy(
            src_ref=src,
            dst_ref=dst,
            send_sem=send_sem.at[index],
            recv_sem=recv_sem.at[index],
            device_id=device,
            device_id_type=MESH,
        )

    out1 = remote(raw, near1, 0, at_sector(-1))
    relay = remote(near1, near2, 1, at_sector(-1))
    out3 = remote(raw.at[:, pl.ds(0, BLK)], edge, 2, inner)
    ret1 = remote(sent1, back1, 3, at_sector(1))
    ret2 = remote(sent2, back2, 4, at_sector(2))
    ret3 = remote(sent3, back3, 5, outer)

    barrier = pltpu.get_barrier_semaphore()
    for step in (-2, -1, 1):
        pl.semaphore_signal(barrier, inc=1, device_id=at_sector(step), device_id_type=MESH)

    @pl.when(has_inner)
    def _():
        pl.semaphore_signal(barrier, inc=1, device_id=inner, device_id_type=MESH)

    @pl.when(has_outer)
    def _():
        pl.semaphore_signal(barrier, inc=1, device_id=outer, device_id_type=MESH)

    slots = slot_ref[...]
    values = jnp.concatenate(
        [densities_ref[...], points_ref[...], weights_ref[...], jnp.zeros((32 - ROWS, PAN), F32)], axis=0
    )
    pieces = jnp.concatenate([piece.astype(BF16) for piece in split3(values)], axis=0)

    def permute(block, carry):
        rows = pl.ds(pl.multiple_of(block * HALF, HALF), HALF)
        index = lax.broadcasted_iota(jnp.int32, (HALF, PAN), 0) + block * HALF
        hot = jnp.where(index == slots, 1.0, 0.0).astype(BF16)
        moved = dot_minor(pieces, hot)
        raw[:, rows] = (moved[0:32] + moved[32:64] + moved[64:96])[0:ROWS]
        return carry

    lax.fori_loop(0, PAN // HALF, permute, 0, unroll=True)

    stage[...] = jnp.zeros_like(stage)
    pick = jnp.where(
        jnp.logical_and(
            lax.broadcasted_iota(jnp.int32, (DEPTH, 128), 0) >= 88,
            lax.broadcasted_iota(jnp.int32, (DEPTH, 128), 0) < 91,
        ),
        1.0,
        0.0,
    ).astype(BF16)
    for variant in range(4):
        stage_target(stage, raw, variant, PAN)
        for index in range(NBLK):
            turned = stage[:, index * BLK : (index + 1) * BLK].T.astype(BF16)
            target[4 * index + variant] = turned
            target_weight[4 * index + variant] = dot(turned, pick)
    def send_own():
        pl.semaphore_wait(barrier, 3 + jnp.minimum(band, 1) + jnp.minimum(bands - 1 - band, 1))
        out1.start()

        @pl.when(has_inner)
        def _():
            out3.start()

    patient = lax.rem(sector, 32) == 0

    @pl.when(jnp.logical_not(patient))
    def _():
        send_own()

    stage[...] = jnp.zeros_like(stage)

    def load_source(link, raw_ref, count):
        for variant in range(4):
            weight = stage_source(stage, raw_ref, variant, count)
            for index in range(count // HALF):
                cols = slice(index * HALF, (index + 1) * HALF)
                place = ((link * NBLK + index // 2) * 4 + variant) * 2 + index % 2
                source[place] = stage[:, cols].astype(BF16)
                source_weight[place] = weight[:, cols]
        for index in range(count // BLK):
            d = raw_ref[0:16, index * BLK : (index + 1) * BLK]
            high = d.astype(BF16)
            density[link * NBLK + index, 0:16, :] = high
            density[link * NBLK + index, 16:32, :] = (d - high.astype(F32)).astype(BF16)

    load_source(0, raw, PAN)
    result[...] = jnp.zeros_like(result)
    sent1[...] = jnp.zeros_like(sent1)
    sent2[...] = jnp.zeros_like(sent2)
    sent3[...] = jnp.zeros_like(sent3)

    def tile(step, carry):
        link = lax.rem(lax.div(step + 1, 4), 4)
        entry = lax.rem(step + 1, 4)

        @pl.when(step == 3)
        def _():
            @pl.when(patient)
            def _():
                send_own()

            out1.wait_recv()
            relay.start()
            load_source(1, near1, PAN)

        @pl.when(step == 7)
        def _():
            ret1.start()
            relay.wait_recv()
            load_source(2, near2, PAN)

        @pl.when(step == 11)
        def _():
            ret2.start()

            @pl.when(has_outer)
            def _():
                out3.wait_recv()
                load_source(3, edge, BLK)

        @pl.when(jnp.logical_and(step == 15, has_outer))
        def _():
            ret3.start()

        @pl.when(jnp.logical_or(link != 3, has_outer))
        def _():
            target_block = pair_ref[0, 0, link, 0, entry]
            source_block = pair_ref[0, 0, link, 1, entry]
            order = order_ref[0, 0, link, entry]
            variants = [jnp.where(order == 3, k, 3) for k in range(3)]
            source_place = link * NBLK + source_block
            for half in range(BLK // HALF):
                block = None
                for k in range(3):
                    points = target[4 * target_block + variants[k]]
                    inner_sum = None
                    for l in range(3):
                        place = (4 * source_place + variants[l]) * 2 + half
                        term = lax.rsqrt(dot(points, source[place])) * source_weight[place]
                        inner_sum = term if inner_sum is None else inner_sum + term
                    scale = target_weight[4 * target_block + variants[k]]
                    term = inner_sum * jnp.concatenate([scale, scale], axis=1)
                    block = term if block is None else block + term
                high = block.astype(BF16)
                tile_high[:, half * HALF : (half + 1) * HALF] = high
                tile_low[:, half * HALF : (half + 1) * HALF] = (block - high.astype(F32)).astype(BF16)
            high = tile_high[...]
            low = tile_low[...]
            far = density[source_place]
            full = dot_minor(far, high)
            forward = full[0:16] + full[16:32] + dot_minor(far[0:16], low)
            for index in range(NBLK):
                result[index] = result[index] + jnp.where(target_block == index, forward, 0.0)

            @pl.when(link != 0)
            def _():
                own = density[target_block]
                full = dot(own, high)
                backward = full[0:16] + full[16:32] + dot(own[0:16], low)

                @pl.when(link == 1)
                def _():
                    for index in range(NBLK):
                        sent1[index] = sent1[index] + jnp.where(source_block == index, backward, 0.0)

                @pl.when(link == 2)
                def _():
                    for index in range(NBLK):
                        sent2[index] = sent2[index] + jnp.where(source_block == index, backward, 0.0)

                @pl.when(link == 3)
                def _():
                    sent3[...] = sent3[...] + backward

        return carry

    lax.fori_loop(0, 16, tile, 0)

    @pl.when(has_inner)
    def _():
        ret3.wait_recv()
        result[0] = result[0] + back3[...]

    ret1.wait_recv()
    ret2.wait_recv()
    for index in range(NBLK):
        out_ref[:, index * BLK : (index + 1) * BLK] = result[index] + back1[index] + back2[index]

    out1.wait_send()
    relay.wait_send()
    ret1.wait_send()
    ret2.wait_send()

    @pl.when(has_inner)
    def _():
        out3.wait_send()

    @pl.when(has_outer)
    def _():
        ret3.wait_send()


def restore(slot_ref, value_ref, out_ref):
    lanes = 128
    for first in range(0, PAN, lanes):
        slots = jnp.broadcast_to(slot_ref[:, first : first + lanes], (NCOL, lanes))
        lane = jnp.bitwise_and(slots, lanes - 1)
        group = jnp.right_shift(slots, 7)
        total = jnp.zeros((NCOL, lanes), F32)
        for index in range(PAN // lanes):
            part = value_ref[:, index * lanes : (index + 1) * lanes]
            found = jnp.take_along_axis(part, lane, axis=1, mode="promise_in_bounds")
            total = jnp.where(group == index, found, total)
        out_ref[:, first : first + lanes] = total


def solution(mesh):
    sectors, bands = mesh.shape["ang"], mesh.shape["rad"]

    def on_device(panel_slot, quad_points, quad_weights, densities, near_pairs, quad_order):
        vmem = pl.BlockSpec(memory_space=pltpu.VMEM)
        smem = pl.BlockSpec(memory_space=pltpu.SMEM)

        def body(*refs):
            kernel(sectors, bands, *refs)

        slots = panel_slot.reshape(1, PAN)
        ordered = pl.pallas_call(
            body,
            name="near_field",
            out_shape=jax.ShapeDtypeStruct((NCOL, PAN), F32),
            in_specs=[smem, smem, vmem, vmem, vmem, vmem],
            out_specs=vmem,
            scratch_shapes=[
                pltpu.VMEM((ROWS, PAN), F32),
                pltpu.VMEM((ROWS, PAN), F32),
                pltpu.VMEM((ROWS, PAN), F32),
                pltpu.VMEM((ROWS, BLK), F32),
                pltpu.VMEM((DEPTH, PAN), F32),
                pltpu.VMEM((NBLK * 4, BLK, DEPTH), BF16),
                pltpu.VMEM((NBLK * 4, BLK, 128), F32),
                pltpu.VMEM((4 * NBLK * 8, DEPTH, HALF), BF16),
                pltpu.VMEM((4 * NBLK * 8, 1, HALF), F32),
                pltpu.VMEM((4 * NBLK, 2 * NCOL, BLK), BF16),
                pltpu.VMEM((BLK, BLK), BF16),
                pltpu.VMEM((BLK, BLK), BF16),
                pltpu.VMEM((NBLK, NCOL, BLK), F32),
                pltpu.VMEM((NBLK, NCOL, BLK), F32),
                pltpu.VMEM((NBLK, NCOL, BLK), F32),
                pltpu.VMEM((NCOL, BLK), F32),
                pltpu.VMEM((NBLK, NCOL, BLK), F32),
                pltpu.VMEM((NBLK, NCOL, BLK), F32),
                pltpu.VMEM((NCOL, BLK), F32),
                pltpu.SemaphoreType.DMA((6,)),
                pltpu.SemaphoreType.DMA((6,)),
            ],
            compiler_params=pltpu.CompilerParams(
                collective_id=0, has_side_effects=True, vmem_limit_bytes=60 * 1024 * 1024
            ),
        )(
            near_pairs,
            quad_order,
            slots,
            quad_points,
            quad_weights,
            densities,
        )
        return pl.pallas_call(
            restore,
            name="restore",
            out_shape=jax.ShapeDtypeStruct((NCOL, PAN), F32),
            in_specs=[vmem, vmem],
            out_specs=vmem,
        )(slots, ordered)

    return jax.shard_map(
        on_device,
        mesh=mesh,
        in_specs=(
            P(("ang", "rad")),
            P(None, ("ang", "rad")),
            P(None, ("ang", "rad")),
            P(None, ("ang", "rad")),
            P("ang", "rad", None, None, None),
            P("ang", "rad", None, None),
        ),
        out_specs=P(None, ("ang", "rad")),
        check_vma=False,
    )
```
